128 devices in a mesh: leaf: 64 (over z, y, x), front: 2 (over core).
Axes of the slice: x: 4, y: 4, z: 4, core: 2. Of those that a mesh axis runs over, the one named last changes fastest.
Arguments:
- leaf_rhs: float32 [2, 32, 64, 2, 256], P(None, None, 'leaf', 'front'), may hold values from -6 to 6
- front_rhs: float32 [2, 32, 64, 1024], P(None, None, 'leaf', 'front'), may hold values from -6 to 6
- leaf_inverse: float32 [64, 2, 256, 256], P('leaf', 'front'), may hold values from -2 to 2, as said below
- coupling: float32 [64, 2, 384, 256], P('leaf', 'front'), may hold values from -0.375 to 0.375
- front_factor: float32 [64, 1024, 1024], P('leaf', 'front'), may hold values from -0.1875 to 0.1875
- front_inverse: float32 [64, 1024, 512], P('leaf', 'front'), may hold values from -2 to 2, as said below
- parent: int32 [64, 2], P('leaf', 'front'), may hold values from 0 to 63
- rows: int32 [64, 2, 384], P('leaf', 'front'), may hold values from 0 to 511, as said below
Outputs:
- leaf_solution: float32 [2, 32, 64, 2, 256], P(None, None, 'leaf', 'front')
- front_solution: float32 [2, 32, 64, 1024], P(None, None, 'leaf', 'front')
The draws below stay inside these ranges and needn't reach their ends.
Inputs may be any that keep to these rules, and one draw needn't show every extreme that they name: `rows`: the 384 row indices of one child are distinct. `leaf_inverse`: each block is a diagonal of 0.8 to 1.25 plus independent entries off and on it. `front_inverse`: each block is a diagonal of 0.8 to 1.25 plus independent entries off and on it.
All inputs are finite; a program needn't handle non-finite values.
Results may differ from the reference program's by a relative error of at most 0.00016.
Values sent between devices are 32-bit elements; how exact they have to be, the bound alone decides.
A program may use at most 64 MiB of HBM per device.

```python
import math
import jax
import jax.numpy as jnp
import numpy as np
from jax import lax

SNODE = 256
CROWS = 384
FORDER = 1024
RHS = 32
BATCHES = 2
PANEL = 512
N_LEAF = 64
N_FRONT = 2


def draw_leaf_inverse(key, part):
    first_key, second_key = jax.random.split(jax.random.fold_in(key, 11))
    count = N_LEAF * N_FRONT
    off_part = jnp.clip(jax.random.normal(first_key, (count, SNODE, SNODE), jnp.float32), -4.0, 4.0)
    off_part = off_part * (0.25 / SNODE ** 0.5)
    diagonal = jnp.exp(jax.random.uniform(second_key, (count, SNODE), jnp.float32, -0.22, 0.22))
    matrix = off_part + diagonal[:, :, None] * jnp.eye(SNODE, dtype=jnp.float32)
    return matrix.reshape(N_LEAF, N_FRONT, SNODE, SNODE)


def draw_front_inverse(key, part):
    first_key, second_key = jax.random.split(jax.random.fold_in(key, 13))
    count = N_LEAF * N_FRONT
    off_part = jnp.clip(jax.random.normal(first_key, (count, PANEL, PANEL), jnp.float32), -4.0, 4.0)
    off_part = off_part * (0.25 / PANEL ** 0.5)
    diagonal = jnp.exp(jax.random.uniform(second_key, (count, PANEL), jnp.float32, -0.22, 0.22))
    matrix = off_part + diagonal[:, :, None] * jnp.eye(PANEL, dtype=jnp.float32)
    return matrix.reshape(N_LEAF, N_FRONT * PANEL, PANEL)


def draw_rows(key, part):
    keys = jax.random.split(jax.random.fold_in(key, 7), N_LEAF * N_FRONT)
    picks = jax.vmap(lambda one_key: jax.random.permutation(one_key, PANEL)[:CROWS])(keys)
    return picks.reshape(N_LEAF, N_FRONT, CROWS).astype(jnp.int32)


def set_ends(drawn, own_key, least, top_value):
    longest = drawn.shape.index(max(drawn.shape))
    spots = []
    for shift in (0, 1):
        where = [jax.random.randint(jax.random.fold_in(own_key, axis), (), 0, length) for axis, length in enumerate(drawn.shape)]
        where[longest] = (where[longest] + shift) % drawn.shape[longest]
        spots.append(tuple(where))
    return drawn.at[spots[0]].set(least).at[spots[1]].set(top_value)


def steps_of(key, dims, cuts, low, largest):
    def one(axis_at, shards_of):
        draws = jax.random.uniform(jax.random.fold_in(jax.random.fold_in(key, 6), axis_at), (shards_of,), jnp.float32, low / len(cuts), largest / len(cuts))
        return jnp.repeat(jnp.exp(draws), dims[axis_at] // shards_of).reshape((-1,) + (1,) * (len(dims) - axis_at - 1))

    loudness = one(*cuts[0])
    for cut in cuts[1:]:
        loudness = loudness * one(*cut)
    return loudness


def rank_bounds(count, skew):
    weights = [(1 << 20) // math.isqrt(standing ** skew) + 1 for standing in range(1, count + 1)]
    width = 1 + sum(weights) // (1 << 30)
    return np.cumsum(np.array([max(1, weight // width) for weight in weights]))


def ranked(key, extent, number_of, lean):
    table = rank_bounds(number_of, lean)
    pick = jax.random.randint(jax.random.fold_in(key, 1), extent, 0, int(table[number_of - 1]))
    standing = jnp.searchsorted(jnp.asarray(table, jnp.int32), pick, side="right")
    return jax.random.permutation(jax.random.fold_in(key, 2), number_of)[standing].astype(jnp.int32)


def centred(rng, extent, width, bound, cuts=(), held_as=jnp.bfloat16):
    values = width * jax.random.normal(rng, extent, jnp.float32)
    if cuts:
        values = values * steps_of(rng, extent, cuts, -0.22, 0.18)
    return jnp.clip(values, -bound, bound).astype(held_as)


def setup_inputs(seed: int = 0) -> dict:
    splits = jax.random.split(jax.random.key(seed), 9)
    return {
        "leaf_rhs": centred(splits[0], (BATCHES, RHS, N_LEAF, N_FRONT, SNODE), 1.0, 6.0, ((2, 64), (3, 2)), jnp.float32),
        "front_rhs": centred(splits[1], (BATCHES, RHS, N_LEAF, FORDER), 1.0, 6.0, ((2, 64), (3, 2)), jnp.float32),
        "leaf_inverse": draw_leaf_inverse(jax.random.fold_in(splits[8], 71), 0),
        "coupling": centred(splits[3], (N_LEAF, N_FRONT, CROWS, SNODE), SNODE ** -0.5, 0.375, ((0, 64), (1, 2)), jnp.float32),
        "front_factor": centred(splits[4], (N_LEAF, FORDER, FORDER), FORDER ** -0.5, 0.1875, ((0, 64), (1, 2)), jnp.float32),
        "front_inverse": draw_front_inverse(jax.random.fold_in(splits[8], 71), 0),
        "parent": set_ends(ranked(splits[6], (N_LEAF, N_FRONT), N_LEAF, 2), jax.random.fold_in(splits[6], 3), 0, N_LEAF - 1).astype(jnp.int32),
        "rows": draw_rows(jax.random.fold_in(splits[8], 71), 0),
    }


highest = lax.Precision.HIGHEST


def reference(leaf_rhs, front_rhs, leaf_inverse, coupling, front_factor, front_inverse, parent, rows):
    leaf_y = jnp.einsum("brlfs,lfts->brlft", leaf_rhs, leaf_inverse, precision=highest)
    update = jnp.einsum("brlfs,lfcs->brlfc", leaf_y, coupling, precision=highest)
    row_onehot = (rows[..., None] == jnp.arange(PANEL, dtype=jnp.int32)).astype(jnp.float32)
    parent_onehot = (parent[..., None] == jnp.arange(N_LEAF, dtype=jnp.int32)).astype(jnp.float32)
    spread_rows = jnp.einsum("brlfc,lfcp->brlfp", update, row_onehot, precision=highest)
    children = jnp.einsum("brlfp,lfg->brgfp", spread_rows, parent_onehot, precision=highest)
    front_load = front_rhs - children.reshape(BATCHES, RHS, N_LEAF, FORDER)
    solved = []
    for block_id in range(N_FRONT):
        first_row = block_id * PANEL
        pending = front_load[..., first_row:first_row + PANEL]
        if block_id > 0:
            prior_y = jnp.concatenate(solved, axis=3)
            pending = pending - jnp.einsum("brgq,gpq->brgp", prior_y, front_factor[:, first_row:first_row + PANEL, :first_row], precision=highest)
        solved.append(jnp.einsum("brgq,gpq->brgp", pending, front_inverse[:, first_row:first_row + PANEL, :], precision=highest))
    front_y = jnp.concatenate(solved, axis=3)
    result = [None] * N_FRONT
    for block_id in reversed(range(N_FRONT)):
        first_row = block_id * PANEL
        pending = front_y[..., first_row:first_row + PANEL]
        if block_id < N_FRONT - 1:
            later_x = jnp.concatenate(result[block_id + 1:], axis=3)
            pending = pending - jnp.einsum("brgp,gpq->brgq", later_x, front_factor[:, first_row + PANEL:, first_row:first_row + PANEL], precision=highest)
        result[block_id] = jnp.einsum("brgp,gpq->brgq", pending, front_inverse[:, first_row:first_row + PANEL, :], precision=highest)
    front_solution = jnp.concatenate(result, axis=3)
    panels = front_solution.reshape(BATCHES, RHS, N_LEAF, N_FRONT, PANEL)
    parent_panel = jnp.einsum("brgfp,lfg->brlfp", panels, parent_onehot, precision=highest)
    gathered_rows = jnp.einsum("brlfp,lfcp->brlfc", parent_panel, row_onehot, precision=highest)
    remain = leaf_y - jnp.einsum("brlfc,lfcs->brlfs", gathered_rows, coupling, precision=highest)
    leaf_solution = jnp.einsum("brlft,lfts->brlfs", remain, leaf_inverse, precision=highest)
    return leaf_solution, front_solution
```

```python
import jax
import jax.numpy as jnp
from jax import lax
from jax.experimental import pallas as pl
from jax.experimental.pallas import tpu as pltpu
from jax.sharding import PartitionSpec as P

MESH = pl.DeviceIdType.MESH
NN = (((1,), (0,)), ((), ()))
NT = (((1,), (1,)), ((), ()))
TN = (((0,), (0,)), ((), ()))
F32, BF16 = jnp.float32, jnp.bfloat16
LANES = 128
GROUP = 8


def split(value):
    high = value.astype(BF16)
    return high, (value - high.astype(F32)).astype(BF16)


def dot(a, b, dims):
    return lax.dot_general(a, b, dims, preferred_element_type=F32)


def dot3(a, b, dims):
    (a_high, a_low), (b_high, b_low) = a, b
    small = dot(a_high, b_low, dims) + dot(a_low, b_high, dims)
    return dot(a_high, b_high, dims) + small


def kernel(
    leaf_rhs, front_rhs, leaf_inv, coupling, factor, inverse, parent, rows,
    leaf_out, front_out,
    rhs_v, load_v, linv_v, coup_v, rows_v, inv0_v, inv1_v, fact_v,
    par_v, recv1, send2, recv2, recv3, send4, recv4, loads,
    inv0_s, inv1_s, fact_s, p_s, g_s, other_s, own_s, last_s,
    in_sem, par_out, par_in, core_out, core_in, load_out, load_in,
    out1, in1, out2, in2, out3, in3, out4, in4,
):
    leaf, core = lax.axis_index("leaf"), lax.axis_index("front")
    panel = inv0_v.shape[0]
    half = recv1.shape[2]
    z, y, x = leaf // 16, (leaf // 4) % 4, leaf % 4

    def near(c):
        return c + 1 - 2 * (c % 2)

    def across(c):
        return 3 - c

    peers = []
    for step in (near, across):
        sx, sy, sz = step(x), step(y), step(z)
        peers.append(
            [
                (sz if k & 4 else z) * 16 + (sy if k & 2 else y) * 4 + (sx if k & 1 else x)
                for k in range(GROUP)
            ]
        )

    def local(src, dst, place):
        return pltpu.make_async_copy(src, dst, in_sem.at[place])

    loads_in = [
        local(leaf_rhs, rhs_v, 0),
        local(leaf_inv, linv_v, 1),
        local(coupling, coup_v, 2),
        local(rows, rows_v, 3),
        local(front_rhs, load_v, 4),
    ]
    for copy in loads_in:
        copy.start()
    left_part = factor.at[:, pl.ds(0, panel)]

    barrier = pltpu.get_barrier_semaphore()
    for group in peers:
        for peer in group[1:]:
            pl.semaphore_signal(barrier, inc=1, device_id=(peer, core), device_id_type=MESH)
    pl.semaphore_signal(barrier, inc=1, device_id=(leaf, 1 - core), device_id_type=MESH)

    @pl.when(core == 0)
    def _():
        local(inverse, inv0_v, 5).start()

    @pl.when(core == 1)
    def _():
        local(inverse, inv1_v, 5).start()
        local(left_part, fact_v, 6).start()

    def remote(src, dst, out_sem, into_sem, peer, side):
        return pltpu.make_async_remote_copy(
            src_ref=src, dst_ref=dst, send_sem=out_sem, recv_sem=into_sem,
            device_id=(peer, side), device_id_type=MESH,
        )

    own_parent = jnp.full((8, LANES), parent[0, 0], jnp.int32)
    par_v[0, 0] = own_parent
    par_v[1, 0] = own_parent
    loads_in[0].wait()
    loads_in[1].wait()
    count = 2 * half
    rhs = jnp.concatenate(
        [rhs_v[pl.ds(0, count, stride=2), :], rhs_v[pl.ds(1, count, stride=2), :]], axis=1
    )
    leaf_inv_parts = split(linv_v[...])
    leaf_y = dot3(split(rhs), leaf_inv_parts, NT)
    leaf_y_parts = split(leaf_y)
    loads_in[2].wait()
    loads_in[3].wait()
    coupling_parts = split(coup_v[...])
    update = dot3(leaf_y_parts, coupling_parts, NT)
    sublane = lax.broadcasted_iota(jnp.int32, (panel, rows_v.shape[1]), 0)
    spread_to = (sublane == rows_v[...]).astype(F32).astype(BF16)
    update_high, update_low = split(update)
    message = dot(update_high, spread_to, NT) + dot(update_low, spread_to, NT)
    for h in range(2):
        recv1[h, 0] = message[h * half : (h + 1) * half]

    pl.semaphore_wait(barrier, 2 * (GROUP - 1) + 1)

    sent = []

    def exchange(h, group, source, target, out_sem, into_sem):
        copies = [None]
        for k in range(1, GROUP):
            copy = remote(source(h, k), target.at[h, k], out_sem.at[h, k], into_sem.at[h, k], peers[group][k], core)
            copy.start()
            copies.append(copy)
        sent.extend(copies[1:])
        return copies

    tables = [
        exchange(h, h, lambda h, k: par_v.at[h, 0], par_v, par_out, par_in) for h in range(2)
    ]
    first = [
        exchange(h, h, lambda h, k: recv1.at[h, 0], recv1, out1, in1) for h in range(2)
    ]

    def core_copy(src, dst, place):
        return remote(src, dst, core_out.at[place], core_in.at[place], leaf, 1 - core)

    @pl.when(core == 0)
    def _():
        core_copy(inverse, inv0_v, 0).start()

    @pl.when(core == 1)
    def _():
        core_copy(inverse, inv1_v, 1).start()
        core_copy(left_part, fact_v, 2).start()

    base = dot3(leaf_y_parts, leaf_inv_parts, NN)
    both = split(dot3(coupling_parts, leaf_inv_parts, NN))
    last = split(dot(spread_to, both[0], NN) + dot(spread_to, both[1], NN))
    last_s[0] = last[0]
    last_s[1] = last[1]

    block = 128

    def keep(where, value, at):
        high, low = split(value)
        where[0, at, :] = high
        where[1, at, :] = low

    def spans(i):
        return pl.ds(pl.multiple_of(i * block, block), block)

    def whole(ref):
        return ref[0], ref[1]

    def by_rows(ref, at):
        return ref[0, at, :], ref[1, at, :]

    def by_columns(ref, at):
        return ref[0, :, at], ref[1, :, at]

    def over(body):
        @pl.loop(0, panel // block)
        def _(i):
            body(spans(i))

    @pl.when(core == 0)
    def _():
        local(inverse, inv0_v, 5).wait()
        core_copy(inverse, inv1_v, 1).wait_recv()
        core_copy(left_part, fact_v, 2).wait_recv()

    @pl.when(core == 1)
    def _():
        local(inverse, inv1_v, 5).wait()
        local(left_part, fact_v, 6).wait()
        core_copy(inverse, inv0_v, 0).wait_recv()

    def split_all(at):
        keep(inv0_s, inv0_v[at, :], at)
        keep(inv1_s, inv1_v[at, :], at)
        keep(fact_s, fact_v[at, :], at)

    over(split_all)
    over(lambda at: keep(p_s, dot3(by_rows(fact_s, at), whole(inv0_s), NN), at))
    over(lambda at: keep(g_s, dot3(by_columns(inv1_s, at), whole(inv1_s), TN), at))

    @pl.when(core == 0)
    def _():
        over(lambda at: keep(other_s, -dot3(by_rows(g_s, at), whole(p_s), NN), at))

    @pl.when(core == 1)
    def _():
        over(lambda at: keep(other_s, -dot3(by_columns(p_s, at), whole(g_s), TN), at))

    groups_of_rows = half // 8

    def sums(source, h, group, into_own, into_others):
        @pl.loop(0, groups_of_rows)
        def _(i):
            at = pl.ds(pl.multiple_of(i * 8, 8), 8)
            marks = [par_v[h, k] for k in range(GROUP)]
            for c in range(panel // LANES):
                lanes = pl.ds(c * LANES, LANES)
                values = [source[h, k, at, lanes] for k in range(GROUP)]
                for j in range(GROUP):
                    total = jnp.zeros((8, LANES), F32)
                    for k in range(GROUP):
                        total = total + jnp.where(marks[k] == peers[group][j], values[k], 0.0)
                    if j == 0:
                        into_own[h, 0, at, lanes] = total
                    else:
                        into_others[h, j, at, lanes] = total

    second = []
    for h in range(2):
        for k in range(1, GROUP):
            tables[h][k].wait_recv()
            first[h][k].wait_recv()
        sums(recv1, h, 1 - h, recv2, send2)
        second.append(exchange(h, 1 - h, lambda h, k: send2.at[h, k], recv2, out2, in2))

    @pl.when(core == 0)
    def _():
        def finish(at):
            value = dot3(by_columns(inv0_s, at), whole(inv0_s), TN)
            keep(own_s, value - dot3(by_columns(p_s, at), whole(other_s), TN), at)

        over(finish)

    @pl.when(core == 1)
    def _():
        def finish(at):
            own_s[0, at, :] = g_s[0, at, :]
            own_s[1, at, :] = g_s[1, at, :]

        over(finish)

    loads_in[4].wait()
    swaps, kept = [], []
    width = panel // LANES
    for h in range(2):
        for k in range(1, GROUP):
            second[h][k].wait_recv()
        total = recv2[h, 0]
        for k in range(1, GROUP):
            total = total + recv2[h, k]
        given = jnp.concatenate(
            [load_v[pl.ds(h * half * width + c, half, stride=width), :] for c in range(width)], axis=1
        )
        load = given - total
        loads[0, h] = load
        swap = remote(loads.at[0, h], loads.at[1, h], load_out.at[h], load_in.at[h], leaf, 1 - core)
        swap.start()
        swaps.append(swap)
        sent.append(swap)
        kept.append(dot3(split(load), whole(own_s), NN))
    third = []
    for h in range(2):
        swaps[h].wait_recv()
        solution = kept[h] + dot3(split(loads[1, h]), whole(other_s), NN)
        recv3[h, 0] = solution
        third.append(exchange(h, 1 - h, lambda h, k: recv3.at[h, 0], recv3, out3, in3))
        for c in range(width):
            front_out[pl.ds(h * half * width + c, half, stride=width), :] = solution[:, c * LANES : (c + 1) * LANES]

    def picks(h, group):
        @pl.loop(0, groups_of_rows)
        def _(i):
            at = pl.ds(pl.multiple_of(i * 8, 8), 8)
            marks = [par_v[h, k] for k in range(GROUP)]
            for c in range(panel // LANES):
                lanes = pl.ds(c * LANES, LANES)
                values = [recv3[h, j, at, lanes] for j in range(GROUP)]
                for k in range(GROUP):
                    picked = jnp.zeros((8, LANES), F32)
                    for j in range(GROUP):
                        picked = jnp.where(marks[k] == peers[group][j], values[j], picked)
                    if k == 0:
                        recv4[h, 0, at, lanes] = picked
                    else:
                        send4[h, k, at, lanes] = picked

    fourth = []
    for h in range(2):
        for k in range(1, GROUP):
            third[h][k].wait_recv()
        picks(h, 1 - h)
        fourth.append(exchange(h, h, lambda h, k: send4.at[h, k], recv4, out4, in4))

    for h in range(2):
        for k in range(1, GROUP):
            fourth[h][k].wait_recv()
        total = recv4[h, 0]
        for k in range(1, GROUP):
            total = total + recv4[h, k]
        result = base[h * half : (h + 1) * half] - dot3(split(total), whole(last_s), NN)
        for c in range(2):
            leaf_out[pl.ds(h * half * 2 + c, half, stride=2), :] = result[:, c * LANES : (c + 1) * LANES]

    for copy in sent:
        copy.wait_send()

    @pl.when(core == 0)
    def _():
        core_copy(inverse, inv0_v, 0).wait_send()

    @pl.when(core == 1)
    def _():
        core_copy(inverse, inv1_v, 1).wait_send()
        core_copy(left_part, fact_v, 2).wait_send()


def on_device(leaf_rhs, front_rhs, leaf_inverse, coupling, front_factor, front_inverse, parent, rows):
    batches, half = leaf_rhs.shape[:2]
    snode, panel = leaf_rhs.shape[4], front_rhs.shape[3]
    count, crows = batches * half, rows.shape[2]
    slots = pltpu.VMEM((2, GROUP, half, panel), F32)
    square = pltpu.VMEM((panel, panel), F32)
    pair = pltpu.VMEM((2, panel, panel), BF16)
    dma = pltpu.SemaphoreType.DMA
    by_group = dma((2, GROUP))
    hbm, vmem = pl.BlockSpec(memory_space=pl.ANY), pl.BlockSpec(memory_space=pltpu.VMEM)
    leaf_x, front_x = pl.pallas_call(
        kernel,
        out_shape=(
            jax.ShapeDtypeStruct((count * snode // LANES, LANES), F32),
            jax.ShapeDtypeStruct((count * panel // LANES, LANES), F32),
        ),
        in_specs=[hbm] * 6 + [pl.BlockSpec(memory_space=pltpu.SMEM), hbm],
        out_specs=(vmem, vmem),
        scratch_shapes=[
            pltpu.VMEM((count * snode // LANES, LANES), F32),
            pltpu.VMEM((count * panel // LANES, LANES), F32),
            pltpu.VMEM((snode, snode), F32),
            pltpu.VMEM((crows, snode), F32),
            pltpu.VMEM((1, crows), jnp.int32),
            square, square, square,
            pltpu.VMEM((2, GROUP, 8, LANES), jnp.int32),
            slots, slots, slots, slots, slots, slots,
            pltpu.VMEM((2, 2, half, panel), F32),
            pair, pair, pair, pair, pair, pair, pair,
            pltpu.VMEM((2, panel, snode), BF16),
            dma((7,)), by_group, by_group, dma((3,)), dma((3,)), dma((2,)), dma((2,)),
        ] + [by_group] * 8,
        compiler_params=pltpu.CompilerParams(
            collective_id=0, has_side_effects=True, vmem_limit_bytes=50 << 20
        ),
    )(
        leaf_rhs.reshape(count * snode // LANES, LANES),
        front_rhs.reshape(count * panel // LANES, LANES),
        leaf_inverse[0, 0],
        coupling[0, 0],
        front_factor[0],
        front_inverse[0],
        parent,
        rows[0],
    )
    return (
        leaf_x.reshape(batches, half, 1, 1, snode),
        front_x.reshape(batches, half, 1, panel),
    )


def solution(mesh):
    placed = (
        P(None, None, "leaf", "front", None),
        P(None, None, "leaf", "front"),
        P("leaf", "front", None, None),
        P("leaf", "front", None, None),
        P("leaf", "front", None),
        P("leaf", "front", None),
        P("leaf", "front"),
        P("leaf", "front", None),
    )
    return jax.shard_map(
        on_device,
        mesh=mesh,
        in_specs=placed,
        out_specs=(P(None, None, "leaf", "front", None), P(None, None, "leaf", "front")),
        check_vma=False,
    )
```

```python
import jax
import jax.numpy as jnp
from jax import lax
from jax.experimental import pallas as pl
from jax.experimental.pallas import tpu as pltpu
from jax.sharding import PartitionSpec as P

MESH = pl.DeviceIdType.MESH
NN = (((1,), (0,)), ((), ()))
NT = (((1,), (1,)), ((), ()))
TN = (((0,), (0,)), ((), ()))
F32, BF16 = jnp.float32, jnp.bfloat16
LANES = 128
GROUP = 8
UNITS = 4
NEXT = (1, 2, 4)
RELAYS = ((2, 1, 3), (4, 2, 6), (1, 4, 5))


def split(value):
    high = value.astype(BF16)
    return high, (value - high.astype(F32)).astype(BF16)


def dot(a, b, dims):
    return lax.dot_general(a, b, dims, preferred_element_type=F32)


def dot3(a, b, dims):
    (a_high, a_low), (b_high, b_low) = a, b
    small = dot(a_high, b_low, dims) + dot(a_low, b_high, dims)
    return dot(a_high, b_high, dims) + small


def thin_dot3(a, b, dims):
    a_high, a_low = split(a)
    rows = a.shape[0]
    wide = dot(jnp.concatenate([a_high, a_low], axis=0), b[0], dims)
    return wide[:rows] + (wide[rows:] + dot(a_high, b[1], dims))


def kernel(
    leaf_rhs, front_rhs, leaf_inv, coupling, factor, inverse, parent, rows,
    leaf_out, front_out,
    rhs_v, load_v, linv_v, coup_v, rows_v, inv0_v, inv1_v, fact_v, par_s,
    par_v, recv1, send2, part2, recv2, recv3, send4, part4, recv4, loads, kept, base_v,
    inv0_s, inv1_s, fact_s, p_s, g_s, own_s, last_s,
    in_sem, par_out, par_in, core_out, core_in, load_out, load_in,
    out1, in1, out2, in2, out3, in3, out4, in4,
):
    leaf, core = lax.axis_index("leaf"), lax.axis_index("front")
    panel = inv0_v.shape[0]
    part = recv1.shape[3]
    unit = 2 * part
    count = UNITS * unit
    width = panel // LANES
    z, y, x = leaf // 16, (leaf // 4) % 4, leaf % 4

    def near(c):
        return c + 1 - 2 * (c % 2)

    def across(c):
        return 3 - c

    peers = []
    for step in (near, across):
        sx, sy, sz = step(x), step(y), step(z)
        peers.append(
            [
                (sz if k & 4 else z) * 16 + (sy if k & 2 else y) * 4 + (sx if k & 1 else x)
                for k in range(GROUP)
            ]
        )

    def local(src, dst, place):
        return pltpu.make_async_copy(src, dst, in_sem.at[place])

    loads_in = [
        local(leaf_rhs, rhs_v, 0),
        local(leaf_inv, linv_v, 1),
        local(parent, par_s, 7),
        local(coupling, coup_v, 2),
        local(rows, rows_v, 3),
    ]
    for copy in loads_in:
        copy.start()
    load_copy = local(front_rhs, load_v, 4)
    left_part = factor.at[:, pl.ds(0, panel)]

    barrier = pltpu.get_barrier_semaphore()
    for group in peers:
        for peer in group[1:]:
            pl.semaphore_signal(barrier, inc=1, device_id=(peer, core), device_id_type=MESH)
    pl.semaphore_signal(barrier, inc=1, device_id=(leaf, 1 - core), device_id_type=MESH)

    @pl.when(core == 0)
    def _():
        local(inverse, inv0_v, 5).start()

    @pl.when(core == 1)
    def _():
        local(inverse, inv1_v, 5).start()
        local(left_part, fact_v, 6).start()

    load_copy.start()

    def remote(src, dst, out_sem, into_sem, peer, side):
        return pltpu.make_async_remote_copy(
            src_ref=src, dst_ref=dst, send_sem=out_sem, recv_sem=into_sem,
            device_id=(peer, side), device_id_type=MESH,
        )

    for copy in loads_in:
        copy.wait()
    own_parent = jnp.full((8, LANES), par_s[0, 0], jnp.int32)
    par_v[0, 0] = own_parent
    par_v[1, 0] = own_parent
    rhs = jnp.concatenate(
        [rhs_v[pl.ds(0, count, stride=2), :], rhs_v[pl.ds(1, count, stride=2), :]], axis=1
    )
    leaf_inv_parts = split(linv_v[...])
    leaf_y = thin_dot3(rhs, leaf_inv_parts, NT)
    coupling_parts = split(coup_v[...])
    update = thin_dot3(leaf_y, coupling_parts, NT)
    sublane = lax.broadcasted_iota(jnp.int32, (panel, rows_v.shape[1]), 0)
    spread_to = (sublane == rows_v[...]).astype(F32).astype(BF16)
    update_parts = jnp.concatenate(split(update), axis=0)
    message = dot(update_parts, spread_to, NT)
    message = message[:count] + message[count:]
    for u in range(UNITS):
        for s in range(2):
            first_row = u * unit + s * part
            recv1[u, s, 0] = message[first_row : first_row + part]

    pl.semaphore_wait(barrier, 2 * (GROUP - 1) + 1)

    def start(src, dst, out_sem, into_sem, group, k):
        remote(src, dst, out_sem, into_sem, peers[group][k], core).start()

    def arrived(ref, sem):
        pltpu.make_async_copy(ref, ref, sem).wait()

    def gather_start(u, s, group, blocks, out_sem, in_sems):
        for k in NEXT + (7,):
            start(blocks.at[u, s, 0], blocks.at[u, s, k], out_sem, in_sems.at[u, s, k], group, k)

    def gather_relay(u, s, group, blocks, out_sem, in_sems):
        for held, to, there in RELAYS:
            arrived(blocks.at[u, s, held], in_sems.at[u, s, held])
            start(blocks.at[u, s, held], blocks.at[u, s, there], out_sem, in_sems.at[u, s, there], group, to)

    def gather_end(u, s, blocks, in_sems):
        for k in (3, 5, 6, 7):
            arrived(blocks.at[u, s, k], in_sems.at[u, s, k])

    def reduce_start(u, s, group, blocks, parts, sums, out_sem, in_sems):
        for held, to, there in RELAYS:
            start(blocks.at[u, s, there], parts.at[u, s, held], out_sem, in_sems.at[u, s, there], group, to)
        start(blocks.at[u, s, 7], sums.at[u, s, 7], out_sem, in_sems.at[u, s, 7], group, 7)

    def reduce_relay(u, s, group, blocks, parts, sums, out_sem, in_sems):
        for held, to, there in RELAYS:
            arrived(parts.at[u, s, held], in_sems.at[u, s, there])
            blocks[u, s, held] = blocks[u, s, held] + parts[u, s, held]
            start(blocks.at[u, s, held], sums.at[u, s, held], out_sem, in_sems.at[u, s, held], group, held)

    def reduce_end(u, sums, in_sems):
        totals = []
        for s in range(2):
            for k in NEXT + (7,):
                arrived(sums.at[u, s, k], in_sems.at[u, s, k])
            total = sums[u, s, 0]
            for k in NEXT + (7,):
                total = total + sums[u, s, k]
            totals.append(total)
        return jnp.concatenate(totals, axis=0)

    for s in range(2):
        for k in range(1, GROUP):
            start(par_v.at[s, 0], par_v.at[s, k], par_out, par_in.at[s, k], s, k)
    for u in range(UNITS):
        for s in range(2):
            gather_start(u, s, s, recv1, out1, in1)

    def core_copy(src, dst, place):
        return remote(src, dst, core_out.at[place], core_in.at[place], leaf, 1 - core)

    @pl.when(core == 0)
    def _():
        core_copy(inverse, inv0_v, 0).start()

    @pl.when(core == 1)
    def _():
        core_copy(inverse, inv1_v, 1).start()
        core_copy(left_part, fact_v, 2).start()

    block = 128

    def keep(where, value, at):
        high, low = split(value)
        where[0, at, :] = high
        where[1, at, :] = low

    def spans(i):
        return pl.ds(pl.multiple_of(i * block, block), block)

    def whole(ref):
        return ref[0], ref[1]

    def by_rows(ref, at):
        return ref[0, at, :], ref[1, at, :]

    def by_columns(ref, at):
        return ref[0, :, at], ref[1, :, at]

    def over(body):
        @pl.loop(0, panel // block)
        def _(i):
            body(spans(i))

    def prepare_last():
        base_v[...] = thin_dot3(leaf_y, leaf_inv_parts, NN)
        both = split(dot3(coupling_parts, leaf_inv_parts, NN))
        last = split(dot(spread_to, both[0], NN) + dot(spread_to, both[1], NN))
        last_s[0] = last[0]
        last_s[1] = last[1]

    def square(source, halves, target):
        over(lambda at: keep(halves, source[at, :], at))
        over(lambda at: keep(target, dot3(by_columns(halves, at), whole(halves), TN), at))

    def prepare_own():
        @pl.when(core == 0)
        def _():
            local(inverse, inv0_v, 5).wait()
            square(inv0_v, inv0_s, own_s)

        @pl.when(core == 1)
        def _():
            local(inverse, inv1_v, 5).wait()
            local(left_part, fact_v, 6).wait()
            square(inv1_v, inv1_s, g_s)
            over(lambda at: keep(fact_s, fact_v[at, :], at))

    def prepare_other():
        @pl.when(core == 0)
        def _():
            core_copy(inverse, inv1_v, 1).wait_recv()
            square(inv1_v, inv1_s, g_s)

        @pl.when(core == 1)
        def _():
            core_copy(inverse, inv0_v, 0).wait_recv()
            over(lambda at: keep(inv0_s, inv0_v[at, :], at))

    def prepare_product():
        @pl.when(core == 0)
        def _():
            core_copy(left_part, fact_v, 2).wait_recv()
            over(lambda at: keep(fact_s, fact_v[at, :], at))

        over(lambda at: keep(p_s, dot3(by_rows(fact_s, at), whole(inv0_s), NN), at))

    def sums(u, s):
        marks = [par_v[s, k] for k in range(GROUP)]
        targets = peers[1 - s]
        for r in range(part // 8):
            at = pl.ds(r * 8, 8)
            for c in range(width):
                lanes = pl.ds(c * LANES, LANES)
                values = [recv1[u, s, k, at, lanes] for k in range(GROUP)]
                for j in range(GROUP):
                    total = jnp.zeros((8, LANES), F32)
                    for k in range(GROUP):
                        total = total + jnp.where(marks[k] == targets[j], values[k], 0.0)
                    if j == 0:
                        recv2[u, s, 0, at, lanes] = total
                    else:
                        send2[u, s, j, at, lanes] = total

    def picks(u, s):
        marks = [par_v[s, k] for k in range(GROUP)]
        targets = peers[1 - s]
        for r in range(part // 8):
            at = pl.ds(r * 8, 8)
            for c in range(width):
                lanes = pl.ds(c * LANES, LANES)
                values = [recv3[u, s, j, at, lanes] for j in range(GROUP)]
                for k in range(GROUP):
                    picked = jnp.zeros((8, LANES), F32)
                    for j in range(GROUP):
                        picked = jnp.where(marks[k] == targets[j], values[j], picked)
                    if k == 0:
                        recv4[u, s, 0, at, lanes] = picked
                    else:
                        send4[u, s, k, at, lanes] = picked

    def relay_update(u):
        for s in range(2):
            gather_relay(u, s, s, recv1, out1, in1)

    def sum_updates(u):
        if u == 0:
            for s in range(2):
                for k in range(1, GROUP):
                    arrived(par_v.at[s, k], par_in.at[s, k])
        for s in range(2):
            gather_end(u, s, recv1, in1)
            sums(u, s)
            reduce_start(u, s, 1 - s, send2, part2, recv2, out2, in2)

    def relay_sums(u):
        for s in range(2):
            reduce_relay(u, s, 1 - s, send2, part2, recv2, out2, in2)

    def swap(u):
        return remote(loads.at[0, u], loads.at[1, u], load_out.at[u], load_in.at[u], leaf, 1 - core)

    def swap_load(u):
        if u == 0:
            load_copy.wait()
        total = reduce_end(u, recv2, in2)
        given = jnp.concatenate(
            [load_v[pl.ds(u * unit * width + c, unit, stride=width), :] for c in range(width)], axis=1
        )
        load = given - total
        loads[0, u] = load
        swap(u).start()

        @pl.when(core == 0)
        def _():
            kept[0, u] = thin_dot3(load, whole(own_s), NN)
            kept[1, u] = thin_dot3(load, whole(p_s), NT)

    def solve(u):
        swap(u).wait_recv()

        def give(solution):
            for s in range(2):
                recv3[u, s, 0] = solution[s * part : (s + 1) * part]
            for c in range(width):
                front_out[pl.ds(u * unit * width + c, unit, stride=width), :] = solution[:, c * LANES : (c + 1) * LANES]

        @pl.when(core == 0)
        def _():
            later = thin_dot3(loads[1, u] - kept[1, u], whole(g_s), NN)
            give(kept[0, u] - thin_dot3(later, whole(p_s), NN))

        @pl.when(core == 1)
        def _():
            pending = loads[0, u] - thin_dot3(loads[1, u], whole(p_s), NT)
            give(thin_dot3(pending, whole(g_s), NN))

        for s in range(2):
            gather_start(u, s, 1 - s, recv3, out3, in3)

    def relay_solution(u):
        for s in range(2):
            gather_relay(u, s, 1 - s, recv3, out3, in3)

    def pick_panels(u):
        for s in range(2):
            gather_end(u, s, recv3, in3)
            picks(u, s)
            reduce_start(u, s, s, send4, part4, recv4, out4, in4)

    def relay_panels(u):
        for s in range(2):
            reduce_relay(u, s, s, send4, part4, recv4, out4, in4)

    def finish(u):
        total = reduce_end(u, recv4, in4)
        result = base_v[pl.ds(u * unit, unit), :] - thin_dot3(total, whole(last_s), NN)
        for c in range(2):
            leaf_out[pl.ds(u * unit * 2 + c, unit, stride=2), :] = result[:, c * LANES : (c + 1) * LANES]

    plan = [(0.0, prepare_last), (0.5, prepare_own), (3.5, prepare_other), (4.3, prepare_product)]
    stages = (
        (2.1, 0.4, relay_update), (4.5, 0.9, sum_updates), (6.8, 0.9, relay_sums), (9.2, 0.9, swap_load),
        (10.4, 0.9, solve), (12.5, 0.9, relay_solution), (14.8, 0.9, pick_panels), (17.0, 0.9, relay_panels),
        (19.4, 0.9, finish),
    )
    for begin, step, stage in stages:
        for u in range(UNITS):
            plan.append((begin + step * u * 4 / UNITS, lambda stage=stage, u=u: stage(u)))
    for _, task in sorted(plan, key=lambda entry: entry[0]):
        task()

    for blocks, sem in ((recv1, out1), (recv2, out2), (recv3, out3), (recv4, out4)):
        seven = blocks.at[:, :, pl.ds(1, GROUP - 1)]
        arrived(seven, sem)
    arrived(par_v.at[:, pl.ds(1, GROUP - 1)], par_out)
    for u in range(UNITS):
        swap(u).wait_send()

    @pl.when(core == 0)
    def _():
        core_copy(inverse, inv0_v, 0).wait_send()

    @pl.when(core == 1)
    def _():
        core_copy(inverse, inv1_v, 1).wait_send()
        core_copy(left_part, fact_v, 2).wait_send()


def on_device(leaf_rhs, front_rhs, leaf_inverse, coupling, front_factor, front_inverse, parent, rows):
    batches, each = leaf_rhs.shape[:2]
    snode, panel = leaf_rhs.shape[4], front_rhs.shape[3]
    count, crows = batches * each, rows.shape[2]
    part = count // (2 * UNITS)
    slots = pltpu.VMEM((UNITS, 2, GROUP, part, panel), F32)
    square = pltpu.VMEM((panel, panel), F32)
    pair = pltpu.VMEM((2, panel, panel), BF16)
    halves = pltpu.VMEM((2, UNITS, 2 * part, panel), F32)
    dma = pltpu.SemaphoreType.DMA
    hbm, vmem = pl.BlockSpec(memory_space=pltpu.HBM), pl.BlockSpec(memory_space=pltpu.VMEM)
    leaf_x, front_x = pl.pallas_call(
        kernel,
        out_shape=(
            jax.ShapeDtypeStruct((count * snode // LANES, LANES), F32),
            jax.ShapeDtypeStruct((count * panel // LANES, LANES), F32),
        ),
        in_specs=[hbm] * 8,
        out_specs=(vmem, vmem),
        scratch_shapes=[
            pltpu.VMEM((count * snode // LANES, LANES), F32),
            pltpu.VMEM((count * panel // LANES, LANES), F32),
            pltpu.VMEM((snode, snode), F32),
            pltpu.VMEM((crows, snode), F32),
            pltpu.VMEM((1, crows), jnp.int32),
            square, square, square,
            pltpu.SMEM((1, 1), jnp.int32),
            pltpu.VMEM((2, GROUP, 8, LANES), jnp.int32),
            slots, slots, slots, slots, slots, slots, slots, slots,
            halves, halves,
            pltpu.VMEM((count, snode), F32),
            pair, pair, pair, pair, pair, pair,
            pltpu.VMEM((2, panel, snode), BF16),
            dma((8,)), dma, dma((2, GROUP)), dma((3,)), dma((3,)), dma((UNITS,)), dma((UNITS,)),
        ] + [dma, dma((UNITS, 2, GROUP))] * 4,
        compiler_params=pltpu.CompilerParams(
            collective_id=0, has_side_effects=True, vmem_limit_bytes=67043328
        ),
    )(
        leaf_rhs.reshape(count * snode // LANES, LANES),
        front_rhs.reshape(count * panel // LANES, LANES),
        leaf_inverse[0, 0],
        coupling[0, 0],
        front_factor[0],
        front_inverse[0],
        parent,
        rows[0],
    )
    return (
        leaf_x.reshape(batches, each, 1, 1, snode),
        front_x.reshape(batches, each, 1, panel),
    )


def solution(mesh):
    placed = (
        P(None, None, "leaf", "front", None),
        P(None, None, "leaf", "front"),
        P("leaf", "front", None, None),
        P("leaf", "front", None, None),
        P("leaf", "front", None),
        P("leaf", "front", None),
        P("leaf", "front"),
        P("leaf", "front", None),
    )
    return jax.shard_map(
        on_device,
        mesh=mesh,
        in_specs=placed,
        out_specs=(P(None, None, "leaf", "front", None), P(None, None, "leaf", "front")),
        check_vma=False,
    )
```

```python
import jax
import jax.numpy as jnp
from jax import lax
from jax.experimental import pallas as pl
from jax.experimental.pallas import tpu as pltpu
from jax.sharding import PartitionSpec as P

MESH = pl.DeviceIdType.MESH
NN = (((1,), (0,)), ((), ()))
NT = (((1,), (1,)), ((), ()))
TN = (((0,), (0,)), ((), ()))
F32, BF16 = jnp.float32, jnp.bfloat16
LANES = 128
GROUP = 8
UNITS = 2
FAR_FIRST = (7, 3, 5, 6, 1, 2, 4)


def split(value):
    high = value.astype(BF16)
    return high, (value - high.astype(F32)).astype(BF16)


def dot(a, b, dims):
    return lax.dot_general(a, b, dims, preferred_element_type=F32)


def dot3(a, b, dims):
    (a_high, a_low), (b_high, b_low) = a, b
    small = dot(a_high, b_low, dims) + dot(a_low, b_high, dims)
    return dot(a_high, b_high, dims) + small


def thin_dot3(a, b, dims):
    a_high, a_low = split(a)
    rows = a.shape[0]
    wide = dot(jnp.concatenate([a_high, a_low], axis=0), b[0], dims)
    return wide[:rows] + (wide[rows:] + dot(a_high, b[1], dims))


def kernel(
    leaf_rhs, front_rhs, leaf_inv, coupling, factor, inverse, rows, parent,
    leaf_out, front_out,
    rhs_v, load_v, linv_v, coup_v, rows_v, inv0_v, inv1_v, fact_v,
    par_v, recv1, send2, recv2, recv3, send4, recv4, loads, kept, base_v,
    inv0_s, inv1_s, fact_s, p_s, g_s, own_s, last_s,
    in_sem, par_out, par_in, core_out, core_in, load_out, load_in,
    out1, in1, out2, in2, out3, in3, out4, in4,
):
    leaf, core = lax.axis_index("leaf"), lax.axis_index("front")
    panel = inv0_v.shape[0]
    part = recv1.shape[3]
    unit = 2 * part
    count = UNITS * unit
    width = panel // LANES
    z, y, x = leaf // 16, (leaf // 4) % 4, leaf % 4

    def near(c):
        return c + 1 - 2 * (c % 2)

    def across(c):
        return 3 - c

    peers = []
    for step in (near, across):
        sx, sy, sz = step(x), step(y), step(z)
        peers.append(
            [
                (sz if k & 4 else z) * 16 + (sy if k & 2 else y) * 4 + (sx if k & 1 else x)
                for k in range(GROUP)
            ]
        )

    def local(src, dst, place):
        return pltpu.make_async_copy(src, dst, in_sem.at[place])

    loads_in = [
        local(leaf_rhs, rhs_v, 0),
        local(leaf_inv, linv_v, 1),
        local(coupling, coup_v, 2),
        local(rows, rows_v, 3),
    ]
    for copy in loads_in:
        copy.start()
    load_copy = local(front_rhs, load_v, 4)
    left_part = factor.at[:, pl.ds(0, panel)]

    barrier = pltpu.get_barrier_semaphore()
    for group in peers:
        for peer in group[1:]:
            pl.semaphore_signal(barrier, inc=1, device_id=(peer, core), device_id_type=MESH)
    pl.semaphore_signal(barrier, inc=1, device_id=(leaf, 1 - core), device_id_type=MESH)

    @pl.when(core == 0)
    def _():
        local(inverse, inv0_v, 5).start()

    @pl.when(core == 1)
    def _():
        local(inverse, inv1_v, 5).start()
        local(left_part, fact_v, 6).start()

    load_copy.start()

    def remote(src, dst, out_sem, into_sem, peer, side):
        return pltpu.make_async_remote_copy(
            src_ref=src, dst_ref=dst, send_sem=out_sem, recv_sem=into_sem,
            device_id=(peer, side), device_id_type=MESH,
        )

    def start(src, dst, out_sem, into_sem, group, k):
        remote(src, dst, out_sem, into_sem, peers[group][k], core).start()

    own_parent = jnp.full((8, LANES), parent[0, 0], jnp.int32)
    par_v[0, 0] = own_parent
    par_v[1, 0] = own_parent
    pl.semaphore_wait(barrier, 2 * (GROUP - 1) + 1)
    for s in range(2):
        for k in FAR_FIRST:
            start(par_v.at[s, 0], par_v.at[s, k], par_out, par_in.at[s, k], s, k)

    for copy in loads_in:
        copy.wait()
    rhs = jnp.concatenate(
        [rhs_v[pl.ds(0, count, stride=2), :], rhs_v[pl.ds(1, count, stride=2), :]], axis=1
    )
    leaf_inv_parts = split(linv_v[...])
    leaf_y = thin_dot3(rhs, leaf_inv_parts, NT)
    coupling_parts = split(coup_v[...])
    update = thin_dot3(leaf_y, coupling_parts, NT)
    sublane = lax.broadcasted_iota(jnp.int32, (panel, rows_v.shape[1]), 0)
    spread_to = (sublane == rows_v[...]).astype(F32).astype(BF16)
    update_parts = jnp.concatenate(split(update), axis=0)
    message = dot(update_parts, spread_to, NT)
    message = message[:count] + message[count:]
    for u in range(UNITS):
        for s in range(2):
            first_row = u * unit + s * part
            recv1[u, s, 0] = message[first_row : first_row + part]

    def arrived(ref, sem):
        pltpu.make_async_copy(ref, ref, sem).wait()

    def gather_start(u, s, group, blocks, out_sem, in_sems):
        for k in FAR_FIRST:
            start(blocks.at[u, s, 0], blocks.at[u, s, k], out_sem, in_sems.at[u, s, k], group, k)

    def gather_end(u, s, blocks, in_sems):
        for k in FAR_FIRST:
            arrived(blocks.at[u, s, k], in_sems.at[u, s, k])

    def reduce_start(u, s, group, blocks, sums, out_sem, in_sems):
        for k in FAR_FIRST:
            start(blocks.at[u, s, k], sums.at[u, s, k], out_sem, in_sems.at[u, s, k], group, k)

    def reduce_end(u, sums, in_sems):
        totals = []
        for s in range(2):
            for k in FAR_FIRST:
                arrived(sums.at[u, s, k], in_sems.at[u, s, k])
            total = sums[u, s, 0]
            for k in range(1, GROUP):
                total = total + sums[u, s, k]
            totals.append(total)
        return jnp.concatenate(totals, axis=0)

    for u in range(UNITS):
        for s in range(2):
            gather_start(u, s, s, recv1, out1, in1)

    def core_copy(src, dst, place):
        return remote(src, dst, core_out.at[place], core_in.at[place], leaf, 1 - core)

    @pl.when(core == 0)
    def _():
        core_copy(inverse, inv0_v, 0).start()

    @pl.when(core == 1)
    def _():
        core_copy(inverse, inv1_v, 1).start()
        core_copy(left_part, fact_v, 2).start()

    block = 128

    def keep(where, value, at):
        high, low = split(value)
        where[0, at, :] = high
        where[1, at, :] = low

    def spans(i):
        return pl.ds(pl.multiple_of(i * block, block), block)

    def whole(ref):
        return ref[0], ref[1]

    def by_rows(ref, at):
        return ref[0, at, :], ref[1, at, :]

    def by_columns(ref, at):
        return ref[0, :, at], ref[1, :, at]

    def over(body):
        @pl.loop(0, panel // block)
        def _(i):
            body(spans(i))

    def prepare_last():
        base_v[...] = thin_dot3(leaf_y, leaf_inv_parts, NN)
        both = split(dot3(coupling_parts, leaf_inv_parts, NN))
        last = split(dot(spread_to, both[0], NN) + dot(spread_to, both[1], NN))
        last_s[0] = last[0]
        last_s[1] = last[1]

    def square(source, halves, target):
        over(lambda at: keep(halves, source[at, :], at))
        over(lambda at: keep(target, dot3(by_columns(halves, at), whole(halves), TN), at))

    def prepare_own():
        @pl.when(core == 0)
        def _():
            local(inverse, inv0_v, 5).wait()
            square(inv0_v, inv0_s, own_s)

        @pl.when(core == 1)
        def _():
            local(inverse, inv1_v, 5).wait()
            local(left_part, fact_v, 6).wait()
            square(inv1_v, inv1_s, g_s)
            over(lambda at: keep(fact_s, fact_v[at, :], at))

    def prepare_other():
        @pl.when(core == 0)
        def _():
            core_copy(inverse, inv1_v, 1).wait_recv()
            square(inv1_v, inv1_s, g_s)

        @pl.when(core == 1)
        def _():
            core_copy(inverse, inv0_v, 0).wait_recv()
            over(lambda at: keep(inv0_s, inv0_v[at, :], at))

    def prepare_product():
        @pl.when(core == 0)
        def _():
            core_copy(left_part, fact_v, 2).wait_recv()
            over(lambda at: keep(fact_s, fact_v[at, :], at))

        over(lambda at: keep(p_s, dot3(by_rows(fact_s, at), whole(inv0_s), NN), at))

    def sums(u, s):
        marks = [par_v[s, k] for k in range(GROUP)]
        targets = peers[1 - s]
        for r in range(part // 8):
            at = pl.ds(r * 8, 8)
            for c in range(width):
                lanes = pl.ds(c * LANES, LANES)
                values = [recv1[u, s, k, at, lanes] for k in range(GROUP)]
                for j in range(GROUP):
                    total = jnp.zeros((8, LANES), F32)
                    for k in range(GROUP):
                        total = total + jnp.where(marks[k] == targets[j], values[k], 0.0)
                    if j == 0:
                        recv2[u, s, 0, at, lanes] = total
                    else:
                        send2[u, s, j, at, lanes] = total

    def picks(u, s):
        marks = [par_v[s, k] for k in range(GROUP)]
        targets = peers[1 - s]
        for r in range(part // 8):
            at = pl.ds(r * 8, 8)
            for c in range(width):
                lanes = pl.ds(c * LANES, LANES)
                values = [recv3[u, s, j, at, lanes] for j in range(GROUP)]
                for k in range(GROUP):
                    picked = jnp.zeros((8, LANES), F32)
                    for j in range(GROUP):
                        picked = jnp.where(marks[k] == targets[j], values[j], picked)
                    if k == 0:
                        recv4[u, s, 0, at, lanes] = picked
                    else:
                        send4[u, s, k, at, lanes] = picked

    def sum_updates(u):
        if u == 0:
            for s in range(2):
                for k in range(1, GROUP):
                    arrived(par_v.at[s, k], par_in.at[s, k])
        for s in range(2):
            gather_end(u, s, recv1, in1)
            sums(u, s)
            reduce_start(u, s, 1 - s, send2, recv2, out2, in2)

    def swap(u):
        return remote(loads.at[0, u], loads.at[1, u], load_out.at[u], load_in.at[u], leaf, 1 - core)

    def swap_load(u):
        if u == 0:
            load_copy.wait()
        total = reduce_end(u, recv2, in2)
        given = jnp.concatenate(
            [load_v[pl.ds(u * unit * width + c, unit, stride=width), :] for c in range(width)], axis=1
        )
        load = given - total
        loads[0, u] = load
        swap(u).start()

        @pl.when(core == 0)
        def _():
            kept[0, u] = thin_dot3(load, whole(own_s), NN)
            kept[1, u] = thin_dot3(load, whole(p_s), NT)

    def solve(u):
        swap(u).wait_recv()

        def give(solution):
            for s in range(2):
                recv3[u, s, 0] = solution[s * part : (s + 1) * part]
            for c in range(width):
                front_out[pl.ds(u * unit * width + c, unit, stride=width), :] = solution[:, c * LANES : (c + 1) * LANES]

        @pl.when(core == 0)
        def _():
            later = thin_dot3(loads[1, u] - kept[1, u], whole(g_s), NN)
            give(kept[0, u] - thin_dot3(later, whole(p_s), NN))

        @pl.when(core == 1)
        def _():
            pending = loads[0, u] - thin_dot3(loads[1, u], whole(p_s), NT)
            give(thin_dot3(pending, whole(g_s), NN))

        for s in range(2):
            gather_start(u, s, 1 - s, recv3, out3, in3)

    def pick_panels(u):
        for s in range(2):
            gather_end(u, s, recv3, in3)
            picks(u, s)
            reduce_start(u, s, s, send4, recv4, out4, in4)

    def finish(u):
        total = reduce_end(u, recv4, in4)
        result = base_v[pl.ds(u * unit, unit), :] - thin_dot3(total, whole(last_s), NN)
        for c in range(2):
            leaf_out[pl.ds(u * unit * 2 + c, unit, stride=2), :] = result[:, c * LANES : (c + 1) * LANES]

    plan = [(0.0, prepare_last), (0.5, prepare_own), (3.5, prepare_other), (5.9, prepare_product)]
    stages = (
        (4.7, 1.2, sum_updates), (9.5, 1.2, swap_load), (10.7, 1.2, solve), (15.8, 1.2, pick_panels), (20.8, 1.2, finish),
    )
    for begin, step, stage in stages:
        for u in range(UNITS):
            plan.append((begin + step * u * 4 / UNITS, lambda stage=stage, u=u: stage(u)))
    for _, task in sorted(plan, key=lambda entry: entry[0]):
        task()

    for blocks, sem in ((recv1, out1), (recv2, out2), (recv3, out3), (recv4, out4)):
        seven = blocks.at[:, :, pl.ds(1, GROUP - 1)]
        arrived(seven, sem)
    arrived(par_v.at[:, pl.ds(1, GROUP - 1)], par_out)
    for u in range(UNITS):
        swap(u).wait_send()

    @pl.when(core == 0)
    def _():
        core_copy(inverse, inv0_v, 0).wait_send()

    @pl.when(core == 1)
    def _():
        core_copy(inverse, inv1_v, 1).wait_send()
        core_copy(left_part, fact_v, 2).wait_send()


def on_device(leaf_rhs, front_rhs, leaf_inverse, coupling, front_factor, front_inverse, parent, rows):
    batches, each = leaf_rhs.shape[:2]
    snode, panel = leaf_rhs.shape[4], front_rhs.shape[3]
    count, crows = batches * each, rows.shape[2]
    part = count // (2 * UNITS)
    slots = pltpu.VMEM((UNITS, 2, GROUP, part, panel), F32)
    square = pltpu.VMEM((panel, panel), F32)
    pair = pltpu.VMEM((2, panel, panel), BF16)
    halves = pltpu.VMEM((2, UNITS, 2 * part, panel), F32)
    dma = pltpu.SemaphoreType.DMA
    hbm, vmem = pl.BlockSpec(memory_space=pltpu.HBM), pl.BlockSpec(memory_space=pltpu.VMEM)
    leaf_x, front_x = pl.pallas_call(
        kernel,
        out_shape=(
            pltpu.VMEM((count * snode // LANES, LANES), F32),
            pltpu.VMEM((count * panel // LANES, LANES), F32),
        ),
        in_specs=[hbm] * 7 + [pl.BlockSpec(memory_space=pltpu.SMEM)],
        out_specs=(vmem, vmem),
        scratch_shapes=[
            pltpu.VMEM((count * snode // LANES, LANES), F32),
            pltpu.VMEM((count * panel // LANES, LANES), F32),
            pltpu.VMEM((snode, snode), F32),
            pltpu.VMEM((crows, snode), F32),
            pltpu.VMEM((1, crows), jnp.int32),
            square, square, square,
            pltpu.VMEM((2, GROUP, 8, LANES), jnp.int32),
            slots, slots, slots, slots, slots, slots,
            halves, halves,
            pltpu.VMEM((count, snode), F32),
            pair, pair, pair, pair, pair, pair,
            pltpu.VMEM((2, panel, snode), BF16),
            dma((8,)), dma, dma((2, GROUP)), dma((3,)), dma((3,)), dma((UNITS,)), dma((UNITS,)),
        ] + [dma, dma((UNITS, 2, GROUP))] * 4,
        compiler_params=pltpu.CompilerParams(
            collective_id=0, has_side_effects=True, vmem_limit_bytes=60 << 20
        ),
    )(
        *(
            pltpu.with_memory_space_constraint(value, pltpu.HBM)
            for value in (
                leaf_rhs.reshape(count * snode // LANES, LANES),
                front_rhs.reshape(count * panel // LANES, LANES),
                leaf_inverse[0, 0],
                coupling[0, 0],
                front_factor[0],
                front_inverse[0],
                rows[0],
            )
        ),
        parent,
    )
    return (
        leaf_x.reshape(batches, each, 1, 1, snode),
        front_x.reshape(batches, each, 1, panel),
    )


def solution(mesh):
    placed = (
        P(None, None, "leaf", "front", None),
        P(None, None, "leaf", "front"),
        P("leaf", "front", None, None),
        P("leaf", "front", None, None),
        P("leaf", "front", None),
        P("leaf", "front", None),
        P("leaf", "front"),
        P("leaf", "front", None),
    )
    return jax.shard_map(
        on_device,
        mesh=mesh,
        in_specs=placed,
        out_specs=(P(None, None, "leaf", "front", None), P(None, None, "leaf", "front")),
        check_vma=False,
    )
```

```python
import jax
import jax.numpy as jnp
from jax import lax
from jax.experimental import pallas as pl
from jax.experimental.pallas import tpu as pltpu
from jax.sharding import PartitionSpec as P

MESH = pl.DeviceIdType.MESH
NN = (((1,), (0,)), ((), ()))
NT = (((1,), (1,)), ((), ()))
TN = (((0,), (0,)), ((), ()))
F32, BF16 = jnp.float32, jnp.bfloat16
LANES = 128
GROUP = 8
UNITS = 2
FIRST, SECOND = (0, 1, 1), (1, 0, 0)
FAR_FIRST = (7, 3, 5, 6, 1, 2, 4)


def split(value):
    high = value.astype(BF16)
    return high, (value - high.astype(F32)).astype(BF16)


def dot(a, b, dims):
    return lax.dot_general(a, b, dims, preferred_element_type=F32)


def dot3(a, b, dims):
    (a_high, a_low), (b_high, b_low) = a, b
    small = dot(a_high, b_low, dims) + dot(a_low, b_high, dims)
    return dot(a_high, b_high, dims) + small


def thin_dot3(a, b, dims):
    a_high, a_low = split(a)
    rows = a.shape[0]
    wide = dot(jnp.concatenate([a_high, a_low], axis=0), b[0], dims)
    return wide[:rows] + (wide[rows:] + dot(a_high, b[1], dims))


def kernel(
    leaf_rhs, front_rhs, leaf_inv, coupling, factor, inverse, rows, parent,
    leaf_out, front_out,
    rhs_v, load_v, linv_v, coup_v, rows_v, inv0_v, inv1_v, fact_v,
    par_v, recv1, send2, recv2, recv3, send4, recv4, loads, kept, base_v,
    inv0_s, inv1_s, fact_s, p_s, g_s, own_s, last_s, onehot_s,
    in_sem, par_out, par_in, core_out, core_in, load_out, load_in,
    out1, in1, out2, in2, out3, in3, out4, in4,
):
    leaf, core = lax.axis_index("leaf"), lax.axis_index("front")
    panel = inv0_v.shape[0]
    part = recv1.shape[3]
    unit = 2 * part
    count = UNITS * unit
    width = panel // LANES
    z, y, x = leaf // 16, (leaf // 4) % 4, leaf % 4

    def near(c):
        return c + 1 - 2 * (c % 2)

    def across(c):
        return 3 - c

    peers = []
    for steps in (FIRST, SECOND):
        sz, sy, sx = (across(c) if far else near(c) for far, c in zip(steps, (z, y, x)))
        peers.append(
            [
                (sz if k & 4 else z) * 16 + (sy if k & 2 else y) * 4 + (sx if k & 1 else x)
                for k in range(GROUP)
            ]
        )

    def local(src, dst, place):
        return pltpu.make_async_copy(src, dst, in_sem.at[place])

    loads_in = [
        local(rows, rows_v, 3),
        local(leaf_rhs, rhs_v, 0),
        local(leaf_inv, linv_v, 1),
        local(coupling, coup_v, 2),
    ]
    load_copy = local(front_rhs, load_v, 4)
    left_part = factor.at[:, pl.ds(0, panel)]

    barrier = pltpu.get_barrier_semaphore()
    for k in FAR_FIRST:
        for group in peers:
            pl.semaphore_signal(barrier, inc=1, device_id=(group[k], core), device_id_type=MESH)
    pl.semaphore_signal(barrier, inc=1, device_id=(leaf, 1 - core), device_id_type=MESH)
    for copy in loads_in:
        copy.start()

    @pl.when(core == 0)
    def _():
        local(inverse, inv0_v, 5).start()

    @pl.when(core == 1)
    def _():
        local(inverse, inv1_v, 5).start()
        local(left_part, fact_v, 6).start()

    load_copy.start()

    def remote(src, dst, out_sem, into_sem, peer, side):
        return pltpu.make_async_remote_copy(
            src_ref=src, dst_ref=dst, send_sem=out_sem, recv_sem=into_sem,
            device_id=(peer, side), device_id_type=MESH,
        )

    def start(src, dst, out_sem, into_sem, group, k):
        remote(src, dst, out_sem, into_sem, peers[group][k], core).start()

    own_parent = jnp.full((8, LANES), parent[0, 0], jnp.int32)
    par_v[0, 0] = own_parent
    par_v[1, 0] = own_parent

    loads_in[0].wait()
    sublane = lax.broadcasted_iota(jnp.int32, (panel, rows_v.shape[1]), 0)
    onehot_s[...] = (sublane == rows_v[...]).astype(F32).astype(BF16)
    loads_in[1].wait()
    rhs = jnp.concatenate(
        [rhs_v[pl.ds(0, count, stride=2), :], rhs_v[pl.ds(1, count, stride=2), :]], axis=1
    )
    loads_in[2].wait()
    leaf_inv_parts = split(linv_v[...])
    leaf_y = thin_dot3(rhs, leaf_inv_parts, NT)
    loads_in[3].wait()
    coupling_parts = split(coup_v[...])
    update = thin_dot3(leaf_y, coupling_parts, NT)
    spread_to = onehot_s[...]
    update_parts = jnp.concatenate(split(update), axis=0)
    message = dot(update_parts, spread_to, NT)
    message = message[:count] + message[count:]
    for u in range(UNITS):
        for s in range(2):
            first_row = u * unit + s * part
            recv1[u, s, 0] = message[first_row : first_row + part]

    pl.semaphore_wait(barrier, 2 * (GROUP - 1) + 1)
    for s in range(2):
        for k in FAR_FIRST:
            start(par_v.at[s, 0], par_v.at[s, k], par_out, par_in.at[s, k], s, k)

    def arrived(ref, sem):
        pltpu.make_async_copy(ref, ref, sem).wait()

    def gather_start(u, s, group, blocks, out_sem, in_sems):
        for k in FAR_FIRST:
            start(blocks.at[u, s, 0], blocks.at[u, s, k], out_sem, in_sems.at[u, s, k], group, k)

    def gather_end(u, s, blocks, in_sems):
        for k in FAR_FIRST:
            arrived(blocks.at[u, s, k], in_sems.at[u, s, k])

    def reduce_send(u, s, group, blocks, sums, out_sem, in_sems):
        def send(k):
            start(blocks.at[u, s, k], sums.at[u, s, k], out_sem, in_sems.at[u, s, k], group, k)

        return send

    def reduce_end(u, sums, in_sems):
        totals = []
        for s in range(2):
            for k in FAR_FIRST:
                arrived(sums.at[u, s, k], in_sems.at[u, s, k])
            total = sums[u, s, 0]
            for k in range(1, GROUP):
                total = total + sums[u, s, k]
            totals.append(total)
        return jnp.concatenate(totals, axis=0)

    for u in range(UNITS):
        for s in range(2):
            gather_start(u, s, s, recv1, out1, in1)

    def core_copy(src, dst, place):
        return remote(src, dst, core_out.at[place], core_in.at[place], leaf, 1 - core)

    @pl.when(core == 0)
    def _():
        core_copy(inverse, inv0_v, 0).start()

    @pl.when(core == 1)
    def _():
        core_copy(inverse, inv1_v, 1).start()
        core_copy(left_part, fact_v, 2).start()

    block = 128

    def keep(where, value, at):
        high, low = split(value)
        where[0, at, :] = high
        where[1, at, :] = low

    def spans(i):
        return pl.ds(pl.multiple_of(i * block, block), block)

    def whole(ref):
        return ref[0], ref[1]

    def by_rows(ref, at):
        return ref[0, at, :], ref[1, at, :]

    def by_columns(ref, at):
        return ref[0, :, at], ref[1, :, at]

    def over(body):
        @pl.loop(0, panel // block)
        def _(i):
            body(spans(i))

    def prepare_last():
        base_v[...] = thin_dot3(leaf_y, leaf_inv_parts, NN)
        both = split(dot3(coupling_parts, leaf_inv_parts, NN))
        last = split(dot(spread_to, both[0], NN) + dot(spread_to, both[1], NN))
        last_s[0] = last[0]
        last_s[1] = last[1]

    def square(source, halves, target):
        over(lambda at: keep(halves, source[at, :], at))
        over(lambda at: keep(target, dot3(by_columns(halves, at), whole(halves), TN), at))

    def prepare_own():
        @pl.when(core == 0)
        def _():
            local(inverse, inv0_v, 5).wait()
            square(inv0_v, inv0_s, own_s)

        @pl.when(core == 1)
        def _():
            local(inverse, inv1_v, 5).wait()
            local(left_part, fact_v, 6).wait()
            square(inv1_v, inv1_s, g_s)
            over(lambda at: keep(fact_s, fact_v[at, :], at))

    def prepare_other():
        @pl.when(core == 0)
        def _():
            core_copy(inverse, inv1_v, 1).wait_recv()
            square(inv1_v, inv1_s, g_s)

        @pl.when(core == 1)
        def _():
            core_copy(inverse, inv0_v, 0).wait_recv()
            over(lambda at: keep(inv0_s, inv0_v[at, :], at))

    def prepare_product():
        @pl.when(core == 0)
        def _():
            core_copy(left_part, fact_v, 2).wait_recv()
            over(lambda at: keep(fact_s, fact_v[at, :], at))

        over(lambda at: keep(p_s, dot3(by_rows(fact_s, at), whole(inv0_s), NN), at))

    def each_slot(own, others, work, send):
        ready = None
        for k in FAR_FIRST:
            work(k, others)
            if ready is not None:
                send(ready)
            ready = k
        work(0, own)
        send(ready)

    def tiles():
        for r in range(part // 8):
            for c in range(width):
                yield pl.ds(r * 8, 8), pl.ds(c * LANES, LANES)

    def sums(u, s, send):
        marks = [par_v[s, k] for k in range(GROUP)]

        def work(j, into):
            chosen = [mark == peers[1 - s][j] for mark in marks]
            for at, lanes in tiles():
                terms = [jnp.where(chosen[k], recv1[u, s, k, at, lanes], 0.0) for k in range(GROUP)]
                while len(terms) > 1:
                    terms = [a + b for a, b in zip(terms[::2], terms[1::2])]
                into[u, s, j, at, lanes] = terms[0]

        each_slot(recv2, send2, work, send)

    def picks(u, s, send):
        marks = [par_v[s, k] for k in range(GROUP)]

        def work(k, into):
            chosen = [marks[k] == peers[1 - s][j] for j in range(GROUP)]
            for at, lanes in tiles():
                picked = jnp.zeros((8, LANES), F32)
                for j in range(GROUP):
                    picked = jnp.where(chosen[j], recv3[u, s, j, at, lanes], picked)
                into[u, s, k, at, lanes] = picked

        each_slot(recv4, send4, work, send)

    def sum_updates(u):
        if u == 0:
            for s in range(2):
                for k in range(1, GROUP):
                    arrived(par_v.at[s, k], par_in.at[s, k])
        for s in range(2):
            gather_end(u, s, recv1, in1)
            sums(u, s, reduce_send(u, s, 1 - s, send2, recv2, out2, in2))

    def swap(u):
        return remote(loads.at[0, u], loads.at[1, u], load_out.at[u], load_in.at[u], leaf, 1 - core)

    def swap_load(u):
        if u == 0:
            load_copy.wait()
        total = reduce_end(u, recv2, in2)
        given = jnp.concatenate(
            [load_v[pl.ds(u * unit * width + c, unit, stride=width), :] for c in range(width)], axis=1
        )
        load = given - total
        loads[0, u] = load
        swap(u).start()

        @pl.when(core == 0)
        def _():
            kept[0, u] = thin_dot3(load, whole(own_s), NN)
            kept[1, u] = thin_dot3(load, whole(p_s), NT)

    def solve(u):
        swap(u).wait_recv()

        def give(solution):
            for s in range(2):
                recv3[u, s, 0] = solution[s * part : (s + 1) * part]
            for c in range(width):
                front_out[pl.ds(u * unit * width + c, unit, stride=width), :] = solution[:, c * LANES : (c + 1) * LANES]

        @pl.when(core == 0)
        def _():
            later = thin_dot3(loads[1, u] - kept[1, u], whole(g_s), NN)
            give(kept[0, u] - thin_dot3(later, whole(p_s), NN))

        @pl.when(core == 1)
        def _():
            pending = loads[0, u] - thin_dot3(loads[1, u], whole(p_s), NT)
            give(thin_dot3(pending, whole(g_s), NN))

        for s in range(2):
            gather_start(u, s, 1 - s, recv3, out3, in3)

    def pick_panels(u):
        for s in range(2):
            gather_end(u, s, recv3, in3)
            picks(u, s, reduce_send(u, s, s, send4, recv4, out4, in4))

    def finish(u):
        total = reduce_end(u, recv4, in4)
        result = base_v[pl.ds(u * unit, unit), :] - thin_dot3(total, whole(last_s), NN)
        for c in range(2):
            leaf_out[pl.ds(u * unit * 2 + c, unit, stride=2), :] = result[:, c * LANES : (c + 1) * LANES]

    plan = [(0.0, prepare_last), (0.5, prepare_own), (3.5, prepare_other), (5.9, prepare_product)]
    stages = (
        (4.7, 1.2, sum_updates), (9.5, 1.2, swap_load), (10.7, 1.2, solve), (15.8, 1.2, pick_panels), (20.8, 1.2, finish),
    )
    for begin, step, stage in stages:
        for u in range(UNITS):
            plan.append((begin + step * u * 4 / UNITS, lambda stage=stage, u=u: stage(u)))
    for _, task in sorted(plan, key=lambda entry: entry[0]):
        task()

    for blocks, sem in ((recv1, out1), (recv2, out2), (recv3, out3), (recv4, out4)):
        seven = blocks.at[:, :, pl.ds(1, GROUP - 1)]
        arrived(seven, sem)
    arrived(par_v.at[:, pl.ds(1, GROUP - 1)], par_out)
    for u in range(UNITS):
        swap(u).wait_send()

    @pl.when(core == 0)
    def _():
        core_copy(inverse, inv0_v, 0).wait_send()

    @pl.when(core == 1)
    def _():
        core_copy(inverse, inv1_v, 1).wait_send()
        core_copy(left_part, fact_v, 2).wait_send()


def put_out(leaf_in, front_in, leaf_out, front_out, sem):
    copies = [
        pltpu.make_async_copy(leaf_in, leaf_out, sem.at[0]),
        pltpu.make_async_copy(front_in, front_out, sem.at[1]),
    ]
    for copy in copies:
        copy.start()
    for copy in copies:
        copy.wait()


def on_device(leaf_rhs, front_rhs, leaf_inverse, coupling, front_factor, front_inverse, parent, rows):
    batches, each = leaf_rhs.shape[:2]
    snode, panel = leaf_rhs.shape[4], front_rhs.shape[3]
    count, crows = batches * each, rows.shape[2]
    part = count // (2 * UNITS)
    slots = pltpu.VMEM((UNITS, 2, GROUP, part, panel), F32)
    square = pltpu.VMEM((panel, panel), F32)
    pair = pltpu.VMEM((2, panel, panel), BF16)
    halves = pltpu.VMEM((2, UNITS, 2 * part, panel), F32)
    dma = pltpu.SemaphoreType.DMA
    hbm, vmem = pl.BlockSpec(memory_space=pltpu.HBM), pl.BlockSpec(memory_space=pltpu.VMEM)
    leaf_x, front_x = pl.pallas_call(
        kernel,
        out_shape=(
            pltpu.VMEM((count * snode // LANES, LANES), F32),
            pltpu.VMEM((count * panel // LANES, LANES), F32),
        ),
        in_specs=[hbm] * 7 + [pl.BlockSpec(memory_space=pltpu.SMEM)],
        out_specs=(vmem, vmem),
        scratch_shapes=[
            pltpu.VMEM((count * snode // LANES, LANES), F32),
            pltpu.VMEM((count * panel // LANES, LANES), F32),
            pltpu.VMEM((snode, snode), F32),
            pltpu.VMEM((crows, snode), F32),
            pltpu.VMEM((1, crows), jnp.int32),
            square, square, square,
            pltpu.VMEM((2, GROUP, 8, LANES), jnp.int32),
            slots, slots, slots, slots, slots, slots,
            halves, halves,
            pltpu.VMEM((count, snode), F32),
            pair, pair, pair, pair, pair, pair,
            pltpu.VMEM((2, panel, snode), BF16),
            pltpu.VMEM((panel, crows), BF16),
            dma((8,)), dma, dma((2, GROUP)), dma((3,)), dma((3,)), dma((UNITS,)), dma((UNITS,)),
        ] + [dma, dma((UNITS, 2, GROUP))] * 4,
        compiler_params=pltpu.CompilerParams(
            collective_id=0, has_side_effects=True, vmem_limit_bytes=60 << 20
        ),
    )(
        *(
            pltpu.with_memory_space_constraint(value, pltpu.HBM)
            for value in (
                leaf_rhs.reshape(count * snode // LANES, LANES),
                front_rhs.reshape(count * panel // LANES, LANES),
                leaf_inverse[0, 0],
                coupling[0, 0],
                front_factor[0],
                front_inverse[0],
                rows[0],
            )
        ),
        parent,
    )
    leaf_x, front_x = pl.pallas_call(
        put_out,
        out_shape=(
            pltpu.HBM((count * snode // LANES, LANES), F32),
            pltpu.HBM((count * panel // LANES, LANES), F32),
        ),
        in_specs=[vmem] * 2,
        out_specs=(hbm, hbm),
        scratch_shapes=[dma((2,))],
    )(*(pltpu.with_memory_space_constraint(value, pltpu.VMEM) for value in (leaf_x, front_x)))
    return (
        leaf_x.reshape(batches, each, 1, 1, snode),
        front_x.reshape(batches, each, 1, panel),
    )


def solution(mesh):
    placed = (
        P(None, None, "leaf", "front", None),
        P(None, None, "leaf", "front"),
        P("leaf", "front", None, None),
        P("leaf", "front", None, None),
        P("leaf", "front", None),
        P("leaf", "front", None),
        P("leaf", "front"),
        P("leaf", "front", None),
    )
    return jax.shard_map(
        on_device,
        mesh=mesh,
        in_specs=placed,
        out_specs=(P(None, None, "leaf", "front", None), P(None, None, "leaf", "front")),
        check_vma=False,
    )
```

```python
import jax
import jax.numpy as jnp
from jax import lax
from jax.experimental import pallas as pl
from jax.experimental.pallas import tpu as pltpu
from jax.sharding import PartitionSpec as P

MESH = pl.DeviceIdType.MESH
NN = (((1,), (0,)), ((), ()))
NT = (((1,), (1,)), ((), ()))
TN = (((0,), (0,)), ((), ()))
F32, BF16 = jnp.float32, jnp.bfloat16
LANES = 128
GROUP = 8
UNITS = 2
FIRST, SECOND = (0, 1, 1), (1, 0, 0)
FAR_FIRST = (7, 3, 5, 6, 1, 2, 4)


def split(value):
    high = value.astype(BF16)
    return high, (value - high.astype(F32)).astype(BF16)


def dot(a, b, dims):
    return lax.dot_general(a, b, dims, preferred_element_type=F32)


def dot3(a, b, dims):
    (a_high, a_low), (b_high, b_low) = a, b
    small = dot(a_high, b_low, dims) + dot(a_low, b_high, dims)
    return dot(a_high, b_high, dims) + small


def thin_dot3(a, b, dims):
    a_high, a_low = split(a)
    rows = a.shape[0]
    wide = dot(jnp.concatenate([a_high, a_low], axis=0), b[0], dims)
    return wide[:rows] + (wide[rows:] + dot(a_high, b[1], dims))


def kernel(
    leaf_rhs, front_rhs, leaf_inv, coupling, factor, inverse, rows, parent,
    leaf_out, front_out,
    rhs_v, load_v, linv_v, coup_v, rows_v, inv0_v, inv1_v, fact_v,
    par_v, recv1, send2, recv2, recv3, send4, recv4, loads, kept, base_v,
    inv0_s, inv1_s, fact_s, p_s, g_s, own_s, other_s, last_s, onehot_s,
    in_sem, par_out, par_in, core_out, core_in, load_out, load_in,
    out1, in1, out2, in2, out3, in3, out4, in4,
):
    leaf, core = lax.axis_index("leaf"), lax.axis_index("front")
    panel = inv0_v.shape[0]
    part = recv1.shape[3]
    unit = 2 * part
    count = UNITS * unit
    width = panel // LANES
    z, y, x = leaf // 16, (leaf // 4) % 4, leaf % 4

    def near(c):
        return c + 1 - 2 * (c % 2)

    def across(c):
        return 3 - c

    peers = []
    for steps in (FIRST, SECOND):
        sz, sy, sx = (across(c) if far else near(c) for far, c in zip(steps, (z, y, x)))
        peers.append(
            [
                (sz if k & 4 else z) * 16 + (sy if k & 2 else y) * 4 + (sx if k & 1 else x)
                for k in range(GROUP)
            ]
        )

    def local(src, dst, place):
        return pltpu.make_async_copy(src, dst, in_sem.at[place])

    loads_in = [
        local(rows, rows_v, 3),
        local(leaf_rhs, rhs_v, 0),
        local(leaf_inv, linv_v, 1),
        local(coupling, coup_v, 2),
    ]
    load_copy = local(front_rhs, load_v, 4)
    left_part = factor.at[:, pl.ds(0, panel)]

    barrier = pltpu.get_barrier_semaphore()
    for k in FAR_FIRST:
        for group in peers:
            pl.semaphore_signal(barrier, inc=1, device_id=(group[k], core), device_id_type=MESH)
    pl.semaphore_signal(barrier, inc=1, device_id=(leaf, 1 - core), device_id_type=MESH)
    for copy in loads_in:
        copy.start()

    @pl.when(core == 0)
    def _():
        local(inverse, inv0_v, 5).start()

    @pl.when(core == 1)
    def _():
        local(inverse, inv1_v, 5).start()
        local(left_part, fact_v, 6).start()

    load_copy.start()

    def remote(src, dst, out_sem, into_sem, peer, side):
        return pltpu.make_async_remote_copy(
            src_ref=src, dst_ref=dst, send_sem=out_sem, recv_sem=into_sem,
            device_id=(peer, side), device_id_type=MESH,
        )

    def start(src, dst, out_sem, into_sem, group, k):
        remote(src, dst, out_sem, into_sem, peers[group][k], core).start()

    own_parent = jnp.full((1, LANES), parent[0, 0], jnp.int32)
    par_v[0, 0] = own_parent
    par_v[1, 0] = own_parent

    loads_in[0].wait()
    sublane = lax.broadcasted_iota(jnp.int32, (panel, rows_v.shape[1]), 0)
    onehot_s[...] = (sublane == rows_v[...]).astype(F32).astype(BF16)
    loads_in[1].wait()
    rhs = jnp.concatenate(
        [rhs_v[pl.ds(0, count, stride=2), :], rhs_v[pl.ds(1, count, stride=2), :]], axis=1
    )
    loads_in[2].wait()
    leaf_inv_parts = split(linv_v[...])
    leaf_y = thin_dot3(rhs, leaf_inv_parts, NT)
    loads_in[3].wait()
    coupling_parts = split(coup_v[...])
    update = thin_dot3(leaf_y, coupling_parts, NT)
    spread_to = onehot_s[...]
    update_parts = jnp.concatenate(split(update), axis=0)
    message = dot(update_parts, spread_to, NT)
    message = message[:count] + message[count:]
    for u in range(UNITS):
        for s in range(2):
            first_row = u * unit + s * part
            recv1[u, s, 0] = message[first_row : first_row + part]

    pl.semaphore_wait(barrier, 2 * (GROUP - 1) + 1)
    for s in range(2):
        for k in FAR_FIRST:
            start(par_v.at[s, 0], par_v.at[s, k], par_out, par_in.at[s, k], s, k)

    def arrived(ref, sem):
        pltpu.make_async_copy(ref, ref, sem).wait()

    def gather_start(u, s, group, blocks, out_sem, in_sems):
        for k in FAR_FIRST:
            start(blocks.at[u, s, 0], blocks.at[u, s, k], out_sem, in_sems.at[u, s, k], group, k)

    def gather_end(u, s, blocks, in_sems):
        for k in FAR_FIRST:
            arrived(blocks.at[u, s, k], in_sems.at[u, s, k])

    def reduce_send(u, s, group, blocks, sums, out_sem, in_sems):
        def send(k):
            start(blocks.at[u, s, k], sums.at[u, s, k], out_sem, in_sems.at[u, s, k], group, k)

        return send

    def reduce_end(u, sums, in_sems):
        totals = []
        for s in range(2):
            for k in FAR_FIRST:
                arrived(sums.at[u, s, k], in_sems.at[u, s, k])
            total = sums[u, s, 0]
            for k in range(1, GROUP):
                total = total + sums[u, s, k]
            totals.append(total)
        return jnp.concatenate(totals, axis=0)

    for u in range(UNITS):
        for s in range(2):
            gather_start(u, s, s, recv1, out1, in1)

    def core_copy(src, dst, place):
        return remote(src, dst, core_out.at[place], core_in.at[place], leaf, 1 - core)

    @pl.when(core == 0)
    def _():
        core_copy(inverse, inv0_v, 0).start()

    @pl.when(core == 1)
    def _():
        core_copy(inverse, inv1_v, 1).start()
        core_copy(left_part, fact_v, 2).start()

    block = 128

    def keep(where, value, at):
        high, low = split(value)
        where[0, at, :] = high
        where[1, at, :] = low

    def spans(i):
        return pl.ds(pl.multiple_of(i * block, block), block)

    def whole(ref):
        return ref[0], ref[1]

    def by_rows(ref, at):
        return ref[0, at, :], ref[1, at, :]

    def by_columns(ref, at):
        return ref[0, :, at], ref[1, :, at]

    def over(body):
        @pl.loop(0, panel // block)
        def _(i):
            body(spans(i))

    def prepare_last():
        base_v[...] = thin_dot3(leaf_y, leaf_inv_parts, NN)
        both = split(dot3(coupling_parts, leaf_inv_parts, NN))
        last = split(dot(spread_to, both[0], NN) + dot(spread_to, both[1], NN))
        last_s[0] = last[0]
        last_s[1] = last[1]

    def square(source, halves, target):
        over(lambda at: keep(halves, source[at, :], at))
        over(lambda at: keep(target, dot3(by_columns(halves, at), whole(halves), TN), at))

    def prepare_own():
        @pl.when(core == 0)
        def _():
            local(inverse, inv0_v, 5).wait()
            square(inv0_v, inv0_s, own_s)

        @pl.when(core == 1)
        def _():
            local(inverse, inv1_v, 5).wait()
            local(left_part, fact_v, 6).wait()
            square(inv1_v, inv1_s, own_s)
            over(lambda at: keep(fact_s, fact_v[at, :], at))

    def prepare_other():
        @pl.when(core == 0)
        def _():
            core_copy(inverse, inv1_v, 1).wait_recv()
            square(inv1_v, inv1_s, g_s)

        @pl.when(core == 1)
        def _():
            core_copy(inverse, inv0_v, 0).wait_recv()
            over(lambda at: keep(inv0_s, inv0_v[at, :], at))

    def prepare_product():
        @pl.when(core == 0)
        def _():
            core_copy(left_part, fact_v, 2).wait_recv()
            over(lambda at: keep(fact_s, fact_v[at, :], at))

        over(lambda at: keep(p_s, dot3(by_rows(fact_s, at), whole(inv0_s), NN), at))

    def prepare_mix():
        @pl.when(core == 0)
        def _():
            over(lambda at: keep(other_s, dot3(by_rows(g_s, at), whole(p_s), NN), at))

            def add(at):
                high, low = by_rows(own_s, at)
                more = dot3(by_columns(p_s, at), whole(other_s), TN)
                keep(own_s, high.astype(F32) + (low.astype(F32) + more), at)

            over(add)

        @pl.when(core == 1)
        def _():
            over(lambda at: keep(other_s, dot3(by_columns(p_s, at), whole(own_s), TN), at))

    def each_slot(own, others, work, send):
        ready = None
        for k in FAR_FIRST:
            work(k, others)
            if ready is not None:
                send(ready)
            ready = k
        work(0, own)
        send(ready)

    def tiles():
        for r in range(part // 8):
            for c in range(width):
                yield pl.ds(r * 8, 8), pl.ds(c * LANES, LANES)

    def sums(u, s, send):
        marks = [jnp.broadcast_to(par_v[s, k], (8, LANES)) for k in range(GROUP)]

        def work(j, into):
            chosen = [mark == peers[1 - s][j] for mark in marks]
            for at, lanes in tiles():
                terms = [jnp.where(chosen[k], recv1[u, s, k, at, lanes], 0.0) for k in range(GROUP)]
                while len(terms) > 1:
                    terms = [a + b for a, b in zip(terms[::2], terms[1::2])]
                into[u, s, j, at, lanes] = terms[0]

        each_slot(recv2, send2, work, send)

    def picks(u, s, send):
        marks = [jnp.broadcast_to(par_v[s, k], (8, LANES)) for k in range(GROUP)]

        def work(k, into):
            chosen = [marks[k] == peers[1 - s][j] for j in range(GROUP)]
            for at, lanes in tiles():
                picked = jnp.zeros((8, LANES), F32)
                for j in range(GROUP):
                    picked = jnp.where(chosen[j], recv3[u, s, j, at, lanes], picked)
                into[u, s, k, at, lanes] = picked

        each_slot(recv4, send4, work, send)

    def sum_updates(u):
        if u == 0:
            for s in range(2):
                for k in range(1, GROUP):
                    arrived(par_v.at[s, k], par_in.at[s, k])
        for s in range(2):
            gather_end(u, s, recv1, in1)
            sums(u, s, reduce_send(u, s, 1 - s, send2, recv2, out2, in2))

    def swap(u):
        return remote(loads.at[0, u], loads.at[1, u], load_out.at[u], load_in.at[u], leaf, 1 - core)

    def swap_load(u):
        if u == 0:
            load_copy.wait()
        total = reduce_end(u, recv2, in2)
        given = jnp.concatenate(
            [load_v[pl.ds(u * unit * width + c, unit, stride=width), :] for c in range(width)], axis=1
        )
        load = given - total
        loads[0, u] = load
        swap(u).start()

        kept[u] = thin_dot3(load, whole(own_s), NN)

    def solve(u):
        swap(u).wait_recv()

        solution = kept[u] - thin_dot3(loads[1, u], whole(other_s), NN)
        for s in range(2):
            recv3[u, s, 0] = solution[s * part : (s + 1) * part]
        for c in range(width):
            front_out[pl.ds(u * unit * width + c, unit, stride=width), :] = solution[:, c * LANES : (c + 1) * LANES]
        for s in range(2):
            gather_start(u, s, 1 - s, recv3, out3, in3)

    def pick_panels(u):
        for s in range(2):
            gather_end(u, s, recv3, in3)
            picks(u, s, reduce_send(u, s, s, send4, recv4, out4, in4))

    def finish(u):
        total = reduce_end(u, recv4, in4)
        result = base_v[pl.ds(u * unit, unit), :] - thin_dot3(total, whole(last_s), NN)
        for c in range(2):
            leaf_out[pl.ds(u * unit * 2 + c, unit, stride=2), :] = result[:, c * LANES : (c + 1) * LANES]

    plan = [(0.5, prepare_own), (3.5, prepare_other), (5.9, prepare_product), (8.4, prepare_mix), (15.0, prepare_last)]
    stages = (
        (4.7, 1.2, sum_updates), (9.5, 1.2, swap_load), (10.7, 1.2, solve), (15.8, 1.2, pick_panels), (20.8, 1.2, finish),
    )
    for begin, step, stage in stages:
        for u in range(UNITS):
            plan.append((begin + step * u * 4 / UNITS, lambda stage=stage, u=u: stage(u)))
    for _, task in sorted(plan, key=lambda entry: entry[0]):
        task()

    for blocks, sem in ((recv1, out1), (recv2, out2), (recv3, out3), (recv4, out4)):
        seven = blocks.at[:, :, pl.ds(1, GROUP - 1)]
        arrived(seven, sem)
    arrived(par_v.at[:, pl.ds(1, GROUP - 1)], par_out)
    for u in range(UNITS):
        swap(u).wait_send()

    @pl.when(core == 0)
    def _():
        core_copy(inverse, inv0_v, 0).wait_send()

    @pl.when(core == 1)
    def _():
        core_copy(inverse, inv1_v, 1).wait_send()
        core_copy(left_part, fact_v, 2).wait_send()


def put_out(leaf_in, front_in, leaf_out, front_out, sem):
    copies = [
        pltpu.make_async_copy(leaf_in, leaf_out, sem.at[0]),
        pltpu.make_async_copy(front_in, front_out, sem.at[1]),
    ]
    for copy in copies:
        copy.start()
    for copy in copies:
        copy.wait()


def on_device(leaf_rhs, front_rhs, leaf_inverse, coupling, front_factor, front_inverse, parent, rows):
    batches, each = leaf_rhs.shape[:2]
    snode, panel = leaf_rhs.shape[4], front_rhs.shape[3]
    count, crows = batches * each, rows.shape[2]
    part = count // (2 * UNITS)
    slots = pltpu.VMEM((UNITS, 2, GROUP, part, panel), F32)
    square = pltpu.VMEM((panel, panel), F32)
    pair = pltpu.VMEM((2, panel, panel), BF16)
    halves = pltpu.VMEM((2, UNITS, 2 * part, panel), F32)
    dma = pltpu.SemaphoreType.DMA
    hbm, vmem = pl.BlockSpec(memory_space=pltpu.HBM), pl.BlockSpec(memory_space=pltpu.VMEM)
    leaf_x, front_x = pl.pallas_call(
        kernel,
        out_shape=(
            pltpu.VMEM((count * snode // LANES, LANES), F32),
            pltpu.VMEM((count * panel // LANES, LANES), F32),
        ),
        in_specs=[hbm] * 7 + [pl.BlockSpec(memory_space=pltpu.SMEM)],
        out_specs=(vmem, vmem),
        scratch_shapes=[
            pltpu.VMEM((count * snode // LANES, LANES), F32),
            pltpu.VMEM((count * panel // LANES, LANES), F32),
            pltpu.VMEM((snode, snode), F32),
            pltpu.VMEM((crows, snode), F32),
            pltpu.VMEM((1, crows), jnp.int32),
            square, square, square,
            pltpu.VMEM((2, GROUP, 1, LANES), jnp.int32),
            slots, slots, slots, slots, slots, slots,
            halves,
            pltpu.VMEM((UNITS, 2 * part, panel), F32),
            pltpu.VMEM((count, snode), F32),
            pair, pair, pair, pair, pair, pair, pair,
            pltpu.VMEM((2, panel, snode), BF16),
            pltpu.VMEM((panel, crows), BF16),
            dma((8,)), dma, dma((2, GROUP)), dma((3,)), dma((3,)), dma((UNITS,)), dma((UNITS,)),
        ] + [dma, dma((UNITS, 2, GROUP))] * 4,
        compiler_params=pltpu.CompilerParams(
            collective_id=0, has_side_effects=True, vmem_limit_bytes=60 << 20
        ),
    )(
        *(
            pltpu.with_memory_space_constraint(value, pltpu.HBM)
            for value in (
                leaf_rhs.reshape(count * snode // LANES, LANES),
                front_rhs.reshape(count * panel // LANES, LANES),
                leaf_inverse[0, 0],
                coupling[0, 0],
                front_factor[0],
                front_inverse[0],
                rows[0],
            )
        ),
        parent,
    )
    leaf_x, front_x = pl.pallas_call(
        put_out,
        out_shape=(
            pltpu.HBM((count * snode // LANES, LANES), F32),
            pltpu.HBM((count * panel // LANES, LANES), F32),
        ),
        in_specs=[vmem] * 2,
        out_specs=(hbm, hbm),
        scratch_shapes=[dma((2,))],
    )(*(pltpu.with_memory_space_constraint(value, pltpu.VMEM) for value in (leaf_x, front_x)))
    return (
        leaf_x.reshape(batches, each, 1, 1, snode),
        front_x.reshape(batches, each, 1, panel),
    )


def solution(mesh):
    placed = (
        P(None, None, "leaf", "front", None),
        P(None, None, "leaf", "front"),
        P("leaf", "front", None, None),
        P("leaf", "front", None, None),
        P("leaf", "front", None),
        P("leaf", "front", None),
        P("leaf", "front"),
        P("leaf", "front", None),
    )
    return jax.shard_map(
        on_device,
        mesh=mesh,
        in_specs=placed,
        out_specs=(P(None, None, "leaf", "front", None), P(None, None, "leaf", "front")),
        check_vma=False,
    )
```
